32 devices in a mesh: seq: 8 (over z, y), tp: 4 (over x, core).
Axes of the slice: x: 2, y: 2, z: 4, core: 2. Of those that a mesh axis runs over, the one named last changes fastest.
Arguments:
- layer_activation: bfloat16 [3072, 2048], P('seq', 'tp'), may hold values from -6 to 6
- sequence_label: int32 [3072], P('seq'), may hold values from 0 to 2, as said below
- sequence_extents: int32 [2], replicated, may hold values from 1 to 1920, as said below
- destination_slots: int32 [2], replicated, may hold values from 0 to 7, as said below
- entry_layernorm_coef: float32 [2048], replicated, may hold values from 0.5 to 1.5
- lagged_blend_coefs: float32 [6, 2048], replicated, may hold values from 0 to 1
- query_matrix: bfloat16 [2048, 2048], P(None, 'tp'), may hold values from -0.125 to 0.125
- lookup_matrix: bfloat16 [2048, 2048], P(None, 'tp'), may hold values from -0.125 to 0.125
- content_matrix: bfloat16 [2048, 2048], P(None, 'tp'), may hold values from -0.125 to 0.125
- readout_matrix: bfloat16 [2048, 2048], P('tp'), may hold values from -0.125 to 0.125
- forgetting_narrow_matrix: bfloat16 [2048, 96], replicated, may hold values from -0.125 to 0.125
- forgetting_widen_matrix: bfloat16 [96, 2048], P(None, 'tp'), may hold values from -2.5 to 2.5
- forgetting_offset: float32 [2048], P('tp'), may hold values from -11 to -3.5
- stepsize_narrow_matrix: bfloat16 [2048, 96], replicated, may hold values from -0.125 to 0.125
- stepsize_widen_matrix: bfloat16 [96, 2048], P(None, 'tp'), may hold values from -0.625 to 0.625
- stepsize_offset: float32 [2048], P('tp'), may hold values from -4 to 4
- gating_narrow_matrix: bfloat16 [2048, 256], replicated, may hold values from -0.125 to 0.125
- gating_widen_matrix: bfloat16 [256, 2048], P(None, 'tp'), may hold values from -0.375 to 0.375
- erasure_lookup_coef: float32 [2048], P('tp'), may hold values from 0.5 to 1.5
- lookup_step_fraction: float32 [2048], P('tp'), may hold values from 0 to 1
- diagonal_reward_coef: float32 [2048], P('tp'), may hold values from -3 to 3
- group_layernorm_coef: float32 [2048], P('tp'), may hold values from 0.5 to 1.5
Outputs:
- mixed: bfloat16 [3072, 2048], P('seq', 'tp')
- final_states: float32 [8, 32, 64, 64], P('seq', 'tp')
- final_rows: bfloat16 [8, 2048], P('seq', 'tp')
The draws below stay inside these ranges and needn't reach their ends.
Inputs may be any that keep to these rules, and one draw needn't show every extreme that they name: `sequence_label`: token p is in prompt 0 for p < sequence_extents[0], in prompt 1 for the next sequence_extents[1] tokens, and padding (2) after them; at least one padding token. `sequence_extents`: one length is exactly 1920, the other at least 768; their sum is under 3072. `destination_slots`: the two owners differ, and one of them is the last index of seq.
All inputs are finite; a program needn't handle non-finite values.
Results may differ from the reference program's by a relative error of at most 0.012.
Values may be sent and summed in bfloat16 or wider, within the bound.
A program may use at most 128 MiB of HBM per device.

```python
import jax
import jax.numpy as jnp
from jax import lax

EMBEDDING_DIM = 2048
NUM_ATTENTIONERS = 32
CHANNELS_PER_ONE = 64
LW = 96
LA = 96
LG = 256
PROMPTS = 2
TOKENS = 3072
N_SEQ = 8
N_TP = 4


def packing_lengths(key):
    base = jax.random.fold_in(key, 7)
    first_key, second_key = jax.random.split(base)
    padding = jax.random.randint(first_key, (), 1, TOKENS // 8 + 1)
    longest = TOKENS * 5 // 8
    shorter = TOKENS - padding - longest
    flipped = jax.random.randint(second_key, (), 0, 2)
    first = jnp.where(flipped == 0, longest, shorter)
    second = jnp.where(flipped == 0, shorter, longest)
    return jnp.stack([first, second]).astype(jnp.int32)


def draw_sequence_extents(key, part):
    return packing_lengths(key)


def draw_sequence_label(key, part):
    sizes = packing_lengths(key)
    places = jnp.arange(TOKENS, dtype=jnp.int32)
    first_end = sizes[0]
    second_end = sizes[0] + sizes[1]
    return ((places >= first_end).astype(jnp.int32) + (places >= second_end).astype(jnp.int32)).astype(jnp.int32)


def draw_destination_slots(key, part):
    base = jax.random.fold_in(key, 11)
    first_key, second_key = jax.random.split(base)
    other = jax.random.randint(first_key, (), 0, N_SEQ - 1)
    last_index = jnp.int32(N_SEQ - 1)
    flipped = jax.random.randint(second_key, (), 0, 2)
    first = jnp.where(flipped == 0, last_index, other)
    second = jnp.where(flipped == 0, other, last_index)
    return jnp.stack([first, second]).astype(jnp.int32)


def draw_forgetting_offset(key, part):
    values = jax.random.uniform(key, (EMBEDDING_DIM,), jnp.float32, -11.0, -3.5)
    return values.astype(jnp.float32)


def level_of(key, shape, pieces, least, largest):
    factor_of = 1.0
    for position, blocks in pieces:
        draws = jax.random.uniform(jax.random.fold_in(jax.random.fold_in(key, 6), position), (blocks,), jnp.float32, least / len(pieces), largest / len(pieces))
        factor_of = factor_of * jnp.repeat(jnp.exp(draws), shape[position] // blocks).reshape((-1,) + (1,) * (len(shape) - 1 - position))
    return factor_of


def scatter_about(key, shape, deviation, reach, cuts=(), kind=jnp.bfloat16):
    factor_of = level_of(key, shape, cuts, -0.22, 0.18) if cuts else 1.0
    array = jax.random.normal(key, shape, jnp.float32) * deviation * factor_of
    return jnp.minimum(jnp.maximum(array, -reach), reach).astype(kind)


def setup_inputs(seed: int = 0) -> dict:
    streams_of = jax.random.split(jax.random.key(seed), 23)
    layer_activation = scatter_about(streams_of[0], (TOKENS, EMBEDDING_DIM), 1.0, 6.0, ((0, 8), (1, 4)))
    sequence_label = draw_sequence_label(jax.random.fold_in(streams_of[22], 71), 0)
    sequence_extents = draw_sequence_extents(jax.random.fold_in(streams_of[22], 71), 0)
    destination_slots = draw_destination_slots(jax.random.fold_in(streams_of[22], 71), 0)
    entry_layernorm_coef = jnp.clip(1.0 + 0.1 * jax.random.normal(streams_of[4], (EMBEDDING_DIM,), jnp.float32), 0.5, 1.5)
    lagged_blend_coefs = jnp.clip(jax.random.uniform(streams_of[5], (6, EMBEDDING_DIM), jnp.float32, 0.0, 1.0), 0.0, 1.0)
    query_matrix = scatter_about(streams_of[6], (EMBEDDING_DIM, EMBEDDING_DIM), EMBEDDING_DIM ** -0.5, 0.125, ((1, 4),))
    lookup_matrix = scatter_about(streams_of[7], (EMBEDDING_DIM, EMBEDDING_DIM), EMBEDDING_DIM ** -0.5, 0.125, ((1, 4),))
    content_matrix = scatter_about(streams_of[8], (EMBEDDING_DIM, EMBEDDING_DIM), EMBEDDING_DIM ** -0.5, 0.125, ((1, 4),))
    readout_matrix = scatter_about(streams_of[9], (EMBEDDING_DIM, EMBEDDING_DIM), EMBEDDING_DIM ** -0.5, 0.125, ((0, 4),))
    forgetting_narrow_matrix = scatter_about(streams_of[10], (EMBEDDING_DIM, LW), EMBEDDING_DIM ** -0.5, 0.125)
    forgetting_widen_matrix = scatter_about(streams_of[11], (LW, EMBEDDING_DIM), (4.0 / LW ** 0.5), 2.5, ((1, 4),))
    forgetting_offset = draw_forgetting_offset(jax.random.fold_in(streams_of[22], 71), 0)
    stepsize_narrow_matrix = scatter_about(streams_of[13], (EMBEDDING_DIM, LA), EMBEDDING_DIM ** -0.5, 0.125)
    stepsize_widen_matrix = scatter_about(streams_of[14], (LA, EMBEDDING_DIM), LA ** -0.5, 0.625, ((1, 4),))
    stepsize_offset = scatter_about(streams_of[15], (EMBEDDING_DIM,), 1.0, 4.0, ((0, 4),), jnp.float32)
    gating_narrow_matrix = scatter_about(streams_of[16], (EMBEDDING_DIM, LG), EMBEDDING_DIM ** -0.5, 0.125)
    gating_widen_matrix = scatter_about(streams_of[17], (LG, EMBEDDING_DIM), LG ** -0.5, 0.375, ((1, 4),))
    erasure_lookup_coef = jnp.clip(0.5 + 1.0 * jax.random.uniform(streams_of[18], (EMBEDDING_DIM,), jnp.float32) ** level_of(streams_of[18], (EMBEDDING_DIM,), ((0, 4),), -0.2, 0.2), 0.5, 1.5)
    lookup_step_fraction = jnp.clip(1.0 * jax.random.uniform(streams_of[19], (EMBEDDING_DIM,), jnp.float32) ** level_of(streams_of[19], (EMBEDDING_DIM,), ((0, 4),), -0.2, 0.2), 0.0, 1.0)
    diagonal_reward_coef = scatter_about(streams_of[20], (EMBEDDING_DIM,), 0.5, 3.0, ((0, 4),), jnp.float32)
    group_layernorm_coef = jnp.clip(1.0 + 0.1 * jax.random.normal(streams_of[21], (EMBEDDING_DIM,), jnp.float32), 0.5, 1.5)
    return {"layer_activation": layer_activation, "sequence_label": sequence_label, "sequence_extents": sequence_extents, "destination_slots": destination_slots, "entry_layernorm_coef": entry_layernorm_coef, "lagged_blend_coefs": lagged_blend_coefs, "query_matrix": query_matrix, "lookup_matrix": lookup_matrix, "content_matrix": content_matrix, "readout_matrix": readout_matrix, "forgetting_narrow_matrix": forgetting_narrow_matrix, "forgetting_widen_matrix": forgetting_widen_matrix, "forgetting_offset": forgetting_offset, "stepsize_narrow_matrix": stepsize_narrow_matrix, "stepsize_widen_matrix": stepsize_widen_matrix, "stepsize_offset": stepsize_offset, "gating_narrow_matrix": gating_narrow_matrix, "gating_widen_matrix": gating_widen_matrix, "erasure_lookup_coef": erasure_lookup_coef, "lookup_step_fraction": lookup_step_fraction, "diagonal_reward_coef": diagonal_reward_coef, "group_layernorm_coef": group_layernorm_coef}


EPS = 1e-05
GROUP_EPS = 0.00064

def reference(layer_activation, sequence_label, sequence_extents, destination_slots, entry_layernorm_coef, lagged_blend_coefs, query_matrix, lookup_matrix, content_matrix, readout_matrix, forgetting_narrow_matrix, forgetting_widen_matrix, forgetting_offset, stepsize_narrow_matrix, stepsize_widen_matrix, stepsize_offset, gating_narrow_matrix, gating_widen_matrix, erasure_lookup_coef, lookup_step_fraction, diagonal_reward_coef, group_layernorm_coef):
    highest = lax.Precision.HIGHEST
    floats = layer_activation.astype(jnp.float32)
    average = lax.optimization_barrier(jnp.mean(floats, axis=1, keepdims=True))
    centred = floats - average
    variance = lax.optimization_barrier(jnp.mean(centred * centred, axis=1, keepdims=True))
    normed = (centred * lax.rsqrt(variance + EPS) * entry_layernorm_coef).astype(jnp.bfloat16)
    normal_f = normed.astype(jnp.float32)
    continues = jnp.concatenate([jnp.zeros((1,), dtype=bool), sequence_label[1:] == sequence_label[:-1]])
    previous = jnp.concatenate([jnp.zeros_like(normal_f[:1]), normal_f[:-1]], axis=0)
    previous = jnp.where(continues[:, None], previous, jnp.zeros_like(previous))
    difference = previous - normal_f

    def blended(which):
        return (normal_f + difference * lagged_blend_coefs[which]).astype(jnp.bfloat16)

    def matmul(left, right):
        return jnp.dot(left, right, preferred_element_type=jnp.float32)
    receptance = matmul(blended(0), query_matrix)
    keys = matmul(blended(2), lookup_matrix)
    values = matmul(blended(3), content_matrix)
    decay_hidden = jnp.tanh(matmul(blended(1), forgetting_narrow_matrix)).astype(jnp.bfloat16)
    learn_hidden = matmul(blended(4), stepsize_narrow_matrix).astype(jnp.bfloat16)
    gate_hidden = jax.nn.sigmoid(matmul(blended(5), gating_narrow_matrix)).astype(jnp.bfloat16)
    log_rate = -jax.nn.softplus(-(forgetting_offset + matmul(decay_hidden, forgetting_widen_matrix))) - 0.5
    decay = jnp.exp(-jnp.exp(log_rate))
    learning = jax.nn.sigmoid(stepsize_offset + matmul(learn_hidden, stepsize_widen_matrix))
    gating_signal = matmul(gate_hidden, gating_widen_matrix)
    number_of_steps = layer_activation.shape[0]
    removal = (keys * erasure_lookup_coef).reshape(number_of_steps, NUM_ATTENTIONERS, CHANNELS_PER_ONE)
    removal = removal * lax.rsqrt(lax.optimization_barrier(jnp.sum(removal * removal, axis=-1, keepdims=True)) + 1e-06)
    written = keys * (1.0 + (learning - 1.0) * lookup_step_fraction)
    split_queries = receptance.reshape(number_of_steps, NUM_ATTENTIONERS, CHANNELS_PER_ONE)
    split_lookups = written.reshape(number_of_steps, NUM_ATTENTIONERS, CHANNELS_PER_ONE)
    split_contents = values.reshape(number_of_steps, NUM_ATTENTIONERS, CHANNELS_PER_ONE)
    head_w = decay.reshape(number_of_steps, NUM_ATTENTIONERS, CHANNELS_PER_ONE)
    head_a = learning.reshape(number_of_steps, NUM_ATTENTIONERS, CHANNELS_PER_ONE)
    ends = (jnp.cumsum(sequence_extents) - 1).astype(jnp.int32)
    positions = jnp.arange(number_of_steps, dtype=jnp.int32)

    def advance(carry, inputs):
        state, saved = carry
        where_now, still, r_now, k_now, v_now, n_now, w_now, a_now = inputs
        state = jnp.where(still, state, jnp.zeros_like(state))
        taken = jnp.einsum('hij,hj->hi', state, -n_now, precision=highest)
        state = state * w_now[:, None, :] + taken[:, :, None] * (n_now * a_now)[:, None, :] + v_now[:, :, None] * k_now[:, None, :]
        readout = jnp.einsum('hij,hj->hi', state, r_now, precision=highest)
        saved = jnp.where((where_now == ends)[:, None, None, None], state[None], saved)
        return ((state, saved), readout)
    start_state = jnp.zeros((NUM_ATTENTIONERS, CHANNELS_PER_ONE, CHANNELS_PER_ONE), jnp.float32)
    start_saved = jnp.zeros((PROMPTS, NUM_ATTENTIONERS, CHANNELS_PER_ONE, CHANNELS_PER_ONE), jnp.float32)
    (last_state, saved), readout = lax.scan(advance, (start_state, start_saved), (positions, continues, split_queries, split_lookups, split_contents, removal, head_w, head_a))
    centre = readout - lax.optimization_barrier(jnp.mean(readout, axis=-1, keepdims=True))
    spread = lax.optimization_barrier(jnp.mean(centre * centre, axis=-1, keepdims=True))
    group_standardized = centre * lax.rsqrt(spread + GROUP_EPS) * group_layernorm_coef.reshape(NUM_ATTENTIONERS, CHANNELS_PER_ONE)
    diagonal_reward = lax.optimization_barrier(jnp.sum(split_queries * split_lookups * diagonal_reward_coef.reshape(NUM_ATTENTIONERS, CHANNELS_PER_ONE), axis=-1, keepdims=True)) * split_contents
    visible_entries = ((group_standardized + diagonal_reward).reshape(number_of_steps, EMBEDDING_DIM) * gating_signal).astype(jnp.bfloat16)
    width = EMBEDDING_DIM // N_TP
    total = floats
    for group in range(N_TP):
        partial_value = matmul(visible_entries[:, group * width:(group + 1) * width], readout_matrix[group * width:(group + 1) * width])
        partial_value = lax.optimization_barrier(partial_value.astype(jnp.bfloat16))
        total = total + partial_value.astype(jnp.float32)
    mixed = total.astype(jnp.bfloat16)
    final_states = jnp.zeros((N_SEQ, NUM_ATTENTIONERS, CHANNELS_PER_ONE, CHANNELS_PER_ONE), jnp.float32)
    final_rows = jnp.zeros((N_SEQ, EMBEDDING_DIM), jnp.bfloat16)
    for prompt in range(PROMPTS):
        final_states = final_states.at[destination_slots[prompt]].set(saved[prompt])
        final_rows = final_rows.at[destination_slots[prompt]].set(normed[ends[prompt]])
    return (mixed, final_states, final_rows)
```

```python
import functools

import jax
import jax.numpy as jnp
from jax import lax
from jax.experimental import pallas as pl
from jax.experimental.pallas import tpu as pltpu
from jax.sharding import PartitionSpec as P

HEAD = 64
PAIR = 128
PROMPTS = 2
CHUNK = 64
EPS = 1e-05
GROUP_EPS = 0.00064
F32 = jnp.float32
BF16 = jnp.bfloat16
NN = (((1,), (0,)), ((), ()))
NT = (((1,), (1,)), ((), ()))
TN = (((0,), (0,)), ((), ()))


def split(x):
    high = x.astype(BF16)
    return high, (x - high.astype(F32)).astype(BF16)


def dot1(a, b, dims=NN):
    return lax.dot_general(a.astype(BF16), b.astype(BF16), dims, preferred_element_type=F32)


def dot3(a, b, dims=NN):
    ah, al = split(a)
    bh, bl = split(b)
    first = lax.dot_general(ah, bh, dims, preferred_element_type=F32)
    second = lax.dot_general(al, bh, dims, preferred_element_type=F32)
    third = lax.dot_general(ah, bl, dims, preferred_element_type=F32)
    return first + (second + third)


def dot_exact_right(a, b):
    ah, al = split(a)
    return lax.dot_general(
        jnp.concatenate([ah, al], axis=1),
        jnp.concatenate([b, b], axis=0),
        NN,
        preferred_element_type=F32,
    )


def head_ones():
    row = lax.broadcasted_iota(jnp.int32, (PAIR, PAIR), 0) // HEAD
    col = lax.broadcasted_iota(jnp.int32, (PAIR, PAIR), 1) // HEAD
    return (row == col).astype(BF16)


def two(x):
    lane = lax.broadcasted_iota(jnp.int32, x.shape, 1)
    zero = jnp.zeros_like(x)
    return jnp.concatenate(
        [jnp.where(lane < HEAD, x, zero), jnp.where(lane >= HEAD, x, zero)], axis=0
    )


def fold(x):
    return x[:HEAD] + x[HEAD:]


def chunk_kernel(
    scal_ref, r_ref, k_ref, v_ref, fl_ref, ll_ref, er_ref, fr_ref, rw_ref, epc_ref, epr_ref,
    y_ref, z_ref, bonus_ref, a_ref, b_ref, maps_ref, run_ref,
):
    c = pl.program_id(0)
    pairs = r_ref.shape[1] // PAIR
    e_in, e_last = scal_ref[c, 0], scal_ref[c, 1]
    inside, moment, e_end = scal_ref[c, 2], scal_ref[c, 3], scal_ref[c, 4]

    row = lax.broadcasted_iota(jnp.int32, (PAIR, PAIR), 0)
    col = lax.broadcasted_iota(jnp.int32, (PAIR, PAIR), 1)
    eye = (row == col).astype(F32)

    @pl.when(c == 0)
    def _():
        maps_ref[...] = jnp.zeros_like(maps_ref)
        for p in range(pairs):
            run_ref[p] = jnp.concatenate([eye, jnp.zeros_like(eye)], axis=0)

    epc = epc_ref[...]
    epc2 = jnp.concatenate([epc, epc], axis=0)
    epr = epr_ref[0, 0:1, :]
    same = (row // HEAD == col // HEAD) & (epc2 == epr)
    strict = same & (row > col)
    diag = same & (row >= col)
    ones = head_ones()
    tri = (
        lax.broadcasted_iota(jnp.int32, (CHUNK, CHUNK), 0)
        >= lax.broadcasted_iota(jnp.int32, (CHUNK, CHUNK), 1)
    ).astype(F32)

    lw_all = -0.6065306597126334 * jax.nn.sigmoid(fl_ref[...])
    lt_all = jnp.dot(tri, lw_all, precision=lax.Precision.HIGHEST, preferred_element_type=F32)
    learn_all = jax.nn.sigmoid(ll_ref[...])
    from_start = (epc2 == e_in).astype(F32)
    chosen = (epc2 == e_last).astype(F32)
    keep = jnp.where(e_last == e_in, 1.0, 0.0).astype(F32)
    sides = [slice(p * PAIR, (p + 1) * PAIR) for p in range(pairs)]
    keys, removals, writtens = [], [], []
    for s in sides:
        k = k_ref[:, s]
        kk = k * er_ref[0:1, s]
        ss = dot_exact_right(kk * kk, ones)
        removals.append(kk * lax.rsqrt(ss + 1e-06))
        writtens.append(k * (1.0 + (learn_all[:, s] - 1.0) * fr_ref[0:1, s]))
    grams, qas, qs, betas, keys, vvs, growths = [], [], [], [], [], [], []
    for p, s in enumerate(sides):
        lw, lt = lw_all[:, s], lt_all[:, s]
        n, w, r, v = removals[p], writtens[p], r_ref[:, s], v_ref[:, s]
        inv = jnp.exp(-lt)
        qa = -n * jnp.exp(lt - lw)
        beta = n * learn_all[:, s] * inv
        key = w * inv
        q = r * jnp.exp(lt)
        bonus_ref[:, s] = dot_exact_right(r * w * rw_ref[0:1, s], ones) * v
        qa2, q2 = two(qa), two(q)
        left = jnp.concatenate([qa2, q2], axis=0)
        right = jnp.concatenate([beta, beta, key, key], axis=0)
        grams.append(dot3(left, right, NT))
        qas.append(qa2)
        qs.append(q2)
        betas.append(two(beta))
        keys.append(two(key))
        vvs.append(two(v))
        growths.append(lt)
    mixes = [jnp.where(strict, g[:PAIR, :PAIR], 0.0) for g in grams]
    inverses = [eye + jnp.where(row // 2 == col // 2, m, 0.0) for m in mixes]
    b = 2
    while b < CHUNK:
        off = (row // (2 * b) == col // (2 * b)) & (row // b != col // b)
        inner = [dot3(jnp.where(off, m, 0.0), x) for m, x in zip(mixes, inverses)]
        inverses = [x + dot3(x, i) for x, i in zip(inverses, inner)]
        b *= 2
    for p, s in enumerate(sides):
        g = grams[p]
        mix_key = jnp.where(strict, g[:PAIR, PAIR:], 0.0)
        read_beta = jnp.where(diag, g[PAIR:, :PAIR], 0.0)
        read_key = jnp.where(diag, g[PAIR:, PAIR:], 0.0)
        kv = dot3(jnp.concatenate([mix_key, read_key], axis=0), vvs[p])
        uw = dot3(
            inverses[p], jnp.concatenate([kv[:PAIR], qas[p] * from_start], axis=1)
        )
        rb = dot3(read_beta, uw)
        z_ref[:, s] = fold(rb[:, :PAIR] + kv[PAIR:])
        y_ref[:, s] = fold(rb[:, PAIR:] + qs[p] * from_start)
        u, w = uw[:, :PAIR], uw[:, PAIR:]
        earlier = run_ref[p]

        def maps(weight, growth, kept):
            bw = betas[p] * (weight * growth)
            kw = keys[p] * (weight * growth)
            both = dot3(uw, bw, TN)
            extra = dot3(vvs[p], kw, TN)
            return both[PAIR:] + eye * (growth * kept), both[:PAIR] + extra

        growth = jnp.exp(growths[p][CHUNK - 1 : CHUNK])
        a_map, b_map = maps(chosen, growth, keep)
        a_ref[0, p] = a_map
        b_ref[0, p] = b_map
        later = dot3(earlier, a_map)
        run_ref[p] = later + jnp.concatenate([jnp.zeros_like(b_map), b_map], axis=0)

        @pl.when(inside == 1)
        def _():
            step = jnp.where(row < CHUNK, row, row - CHUNK)
            here = ((epc2 == e_end) & (step <= moment)).astype(F32)
            pick = lax.broadcasted_iota(jnp.int32, (CHUNK, PAIR), 0) == moment
            grow = jnp.exp(jnp.sum(jnp.where(pick, growths[p], 0.0), axis=0, keepdims=True))
            kept = jnp.where(e_end == e_in, 1.0, 0.0).astype(F32)
            a_end, b_end = maps(here, grow, kept)
            ended = dot3(earlier, a_end)
            maps_ref[0, p] = fold(ended[:PAIR]).astype(BF16)
            maps_ref[2, p] = fold(ended[PAIR:] + b_end).astype(BF16)

        @pl.when(c == pl.num_programs(0) - 1)
        def _():
            maps_ref[1, p] = fold(run_ref[p, PAIR:]).astype(BF16)

        @pl.when((c == pl.num_programs(0) - 1) & (scal_ref[c, 5] == 0))
        def _():
            maps_ref[0, p] = fold(run_ref[p, :PAIR]).astype(BF16)


def read_kernel(
    scal_ref, all_ref, y_ref, z_ref, bonus_ref, gate_ref, gain_ref, a_ref, b_ref,
    vis_ref, final_ref, state_ref, mine_ref,
):
    c = pl.program_id(0)
    pairs = y_ref.shape[1] // PAIR
    count = all_ref.shape[0]
    position = scal_ref[0]

    @pl.when(c == 0)
    def _():
        final_ref[...] = jnp.zeros_like(final_ref)
        state_ref[...] = jnp.zeros_like(state_ref)

        def hop(d, carry):
            @pl.when(d == position)
            def _():
                mine_ref[...] = state_ref[...]

            holds = (d == scal_ref[1]) | (d == scal_ref[2])
            owner = jnp.where(d == scal_ref[1], scal_ref[3], scal_ref[4])

            for p in range(pairs):
                state = state_ref[p]
                high, low = split(state)
                a_map = two(all_ref[d, 0, p].astype(F32)).astype(BF16)
                moved = lax.dot_general(high, a_map, NN, preferred_element_type=F32)
                moved = moved + lax.dot_general(low, a_map, NN, preferred_element_type=F32)

                @pl.when(holds & (owner == position))
                def _():
                    final_ref[p] = fold(moved) + all_ref[d, 2, p].astype(F32)

                local = two(all_ref[d, 1, p].astype(F32))
                state_ref[p] = jnp.where(holds, 0.0, moved) + local
            return carry

        lax.fori_loop(0, count, hop, 0)

    ones = head_ones()
    for p in range(pairs):
        s = slice(p * PAIR, (p + 1) * PAIR)
        state = mine_ref[p]
        out = fold(dot3(two(y_ref[:, s]), state, NT)) + z_ref[:, s]
        mine_ref[p] = dot3(state, a_ref[0, p]) + b_ref[0, p]
        centre = out - dot_exact_right(out, ones) * (1.0 / HEAD)
        spread = dot_exact_right(centre * centre, ones) * (1.0 / HEAD)
        normed = centre * lax.rsqrt(spread + GROUP_EPS) * gain_ref[0:1, s]
        vis_ref[:, s] = ((normed + bonus_ref[:, s]) * gate_ref[:, s]).astype(BF16)


def from_behind(array, axis, by):
    length = lax.axis_size(axis)
    pairs = [(i, i + by) for i in range(length) if 0 <= i + by < length]
    return lax.ppermute(array, axis, pairs)


def matmul(left, right):
    return jnp.dot(left, right, preferred_element_type=F32)


def on_device(
    layer_activation,
    sequence_label,
    sequence_extents,
    destination_slots,
    entry_layernorm_coef,
    lagged_blend_coefs,
    query_matrix,
    lookup_matrix,
    content_matrix,
    readout_matrix,
    forgetting_narrow_matrix,
    forgetting_widen_matrix,
    forgetting_offset,
    stepsize_narrow_matrix,
    stepsize_widen_matrix,
    stepsize_offset,
    gating_narrow_matrix,
    gating_widen_matrix,
    erasure_lookup_coef,
    lookup_step_fraction,
    diagonal_reward_coef,
    group_layernorm_coef,
):
    tokens = layer_activation.shape[0]
    width = query_matrix.shape[1]
    pairs = width // PAIR
    chunks = tokens // CHUNK
    position = lax.axis_index("seq")
    column = lax.axis_index("tp")
    n_seq = lax.axis_size("seq")
    gathered = lax.all_gather(layer_activation, "tp", axis=1, tiled=True)
    floats = gathered.astype(F32)
    average = jnp.mean(floats, axis=1, keepdims=True)
    centred = floats - average
    variance = jnp.mean(centred * centred, axis=1, keepdims=True)
    normed = (centred * lax.rsqrt(variance + EPS) * entry_layernorm_coef).astype(BF16)
    normal_f = normed.astype(F32)
    arrived = from_behind(normed[-1:], "seq", 1)
    bounds = jnp.cumsum(sequence_extents)
    first_token = position * tokens
    before = first_token - 1
    segment_before = (before >= bounds[0]).astype(jnp.int32) + (before >= bounds[1]).astype(
        jnp.int32
    )
    joined = (segment_before == sequence_label[0]) & (position > 0)
    continues = jnp.concatenate([joined[None], sequence_label[1:] == sequence_label[:-1]])
    previous = jnp.concatenate([arrived.astype(F32), normal_f[:-1]], axis=0)
    previous = jnp.where(continues[:, None], previous, jnp.zeros_like(previous))
    difference = previous - normal_f

    def blended(which):
        return (normal_f + difference * lagged_blend_coefs[which]).astype(BF16)

    receptance = matmul(blended(0), query_matrix)
    keys = matmul(blended(2), lookup_matrix)
    values = matmul(blended(3), content_matrix)
    decay_hidden = jnp.tanh(matmul(blended(1), forgetting_narrow_matrix)).astype(BF16)
    learn_hidden = matmul(blended(4), stepsize_narrow_matrix).astype(BF16)
    gate_hidden = jax.nn.sigmoid(matmul(blended(5), gating_narrow_matrix)).astype(BF16)
    forget_logit = forgetting_offset + matmul(decay_hidden, forgetting_widen_matrix)
    learn_logit = stepsize_offset + matmul(learn_hidden, stepsize_widen_matrix)
    gating_signal = matmul(gate_hidden, gating_widen_matrix)

    ends = bounds - 1
    holders = ends // tokens
    epochs = segment_before + jnp.zeros((tokens,), jnp.int32)
    epochs = sequence_label
    before_first = jnp.where(position > 0, segment_before, -1)
    grouped = epochs.reshape(chunks, CHUNK)
    e_last = grouped[:, -1]
    e_in = jnp.concatenate([before_first[None], e_last[:-1]])
    starts = first_token + jnp.arange(chunks, dtype=jnp.int32) * CHUNK
    offsets = ends[None, :] - starts[:, None]
    within = (offsets >= 0) & (offsets < CHUNK)
    inside = jnp.any(within, axis=1).astype(jnp.int32)
    moment = jnp.sum(jnp.where(within, offsets, 0), axis=1)
    e_end = jnp.sum(jnp.where(within, jnp.arange(PROMPTS, dtype=jnp.int32)[None], 0), axis=1)
    device_ends = jnp.broadcast_to(jnp.any(holders == position).astype(jnp.int32), (chunks,))
    scalars = jnp.stack([e_in, e_last, inside, moment, e_end, device_ends], axis=1)
    ep_cols = jnp.broadcast_to(epochs[:, None], (tokens, PAIR))
    ep_rows = jnp.broadcast_to(
        jnp.concatenate([grouped, grouped], axis=1)[:, None, :], (chunks, 8, PAIR)
    )

    def wide():
        return pl.BlockSpec((CHUNK, width), lambda c: (c, 0))

    def coef():
        return pl.BlockSpec((1, width), lambda c: (0, 0))

    def mats():
        return pl.BlockSpec((1, pairs, PAIR, PAIR), lambda c: (c, 0, 0, 0))

    smem = pl.BlockSpec(memory_space=pltpu.SMEM)
    big = jax.ShapeDtypeStruct((tokens, width), F32)
    mat = jax.ShapeDtypeStruct((chunks, pairs, PAIR, PAIR), F32)
    y, z, bonus, a_maps, b_maps, maps = pl.pallas_call(
        chunk_kernel,
        grid=(chunks,),
        in_specs=[smem]
        + [wide()] * 5
        + [coef()] * 3
        + [
            pl.BlockSpec((CHUNK, PAIR), lambda c: (c, 0)),
            pl.BlockSpec((1, 8, PAIR), lambda c: (c, 0, 0)),
        ],
        out_specs=[
            wide(),
            wide(),
            wide(),
            mats(),
            mats(),
            pl.BlockSpec((3, pairs, HEAD, PAIR), lambda c: (0, 0, 0, 0)),
        ],
        out_shape=[big, big, big, mat, mat, jax.ShapeDtypeStruct((3, pairs, HEAD, PAIR), BF16)],
        scratch_shapes=[pltpu.VMEM((pairs, 2 * PAIR, PAIR), F32)],
        compiler_params=pltpu.CompilerParams(vmem_limit_bytes=40 << 20),
    )(
        scalars,
        receptance,
        keys,
        values,
        forget_logit,
        learn_logit,
        erasure_lookup_coef[None],
        lookup_step_fraction[None],
        diagonal_reward_coef[None],
        ep_cols,
        ep_rows,
    )

    local_end = jnp.clip(jnp.max(jnp.where(holders == position, ends - first_token, 0)), 0, tokens - 1)
    row_end = lax.dynamic_slice(normed, (local_end, column * width), (1, width))
    sent = jnp.concatenate(
        [
            maps.reshape(3 * pairs * HEAD, PAIR),
            jnp.pad(row_end.reshape(pairs, PAIR), ((0, 16 - pairs), (0, 0))),
        ],
        axis=0,
    )
    everyone = lax.all_gather(sent, "seq", axis=0, tiled=False)
    all_maps = everyone[:, : 3 * pairs * HEAD].reshape(n_seq, 3, pairs, HEAD, PAIR)
    rows = everyone[:, 3 * pairs * HEAD : 3 * pairs * HEAD + pairs].reshape(n_seq, width)

    facts = jnp.concatenate([position[None], holders, destination_slots]).astype(jnp.int32)
    visible, final_fold = pl.pallas_call(
        read_kernel,
        grid=(chunks,),
        in_specs=[
            smem,
            pl.BlockSpec((n_seq, 3, pairs, HEAD, PAIR), lambda c: (0, 0, 0, 0, 0), pipeline_mode=pl.Buffered(1)),
            wide(),
            wide(),
            wide(),
            wide(),
            coef(),
            mats(),
            mats(),
        ],
        out_specs=[wide(), pl.BlockSpec((pairs, HEAD, PAIR), lambda c: (0, 0, 0))],
        out_shape=[
            jax.ShapeDtypeStruct((tokens, width), BF16),
            jax.ShapeDtypeStruct((pairs, HEAD, PAIR), F32),
        ],
        scratch_shapes=[pltpu.VMEM((pairs, PAIR, PAIR), F32), pltpu.VMEM((pairs, PAIR, PAIR), F32)],
        compiler_params=pltpu.CompilerParams(vmem_limit_bytes=48 << 20),
    )(facts, all_maps, y, z, bonus, gating_signal, group_layernorm_coef[None], a_maps, b_maps)

    final_states = final_fold.reshape(pairs, HEAD, 2, HEAD).transpose(0, 2, 1, 3)
    final_states = final_states.reshape(1, 2 * pairs, HEAD, HEAD)
    final_rows = jnp.zeros((1, width), BF16)
    for prompt in range(PROMPTS):
        got = lax.dynamic_slice(rows, (holders[prompt], 0), (1, width))
        final_rows = jnp.where(position == destination_slots[prompt], got, final_rows)

    partial_value = matmul(visible, readout_matrix)
    summed = lax.psum_scatter(
        partial_value.astype(BF16), "tp", scatter_dimension=1, tiled=True
    ).astype(F32)
    mixed = (summed + layer_activation.astype(F32)).astype(BF16)
    return (mixed, final_states, final_rows)


def solution(mesh):
    return jax.shard_map(
        on_device,
        mesh=mesh,
        in_specs=(
            P("seq", "tp"),
            P("seq"),
            P(),
            P(),
            P(),
            P(),
            P(None, "tp"),
            P(None, "tp"),
            P(None, "tp"),
            P("tp", None),
            P(),
            P(None, "tp"),
            P("tp"),
            P(),
            P(None, "tp"),
            P("tp"),
            P(),
            P(None, "tp"),
            P("tp"),
            P("tp"),
            P("tp"),
            P("tp"),
        ),
        out_specs=(P("seq", "tp"), P("seq", "tp", None, None), P("seq", "tp")),
        check_vma=False,
    )
```

```python
import jax
import jax.numpy as jnp
from jax import lax
from jax.experimental import pallas as pl
from jax.experimental.pallas import tpu as pltpu
from jax.sharding import PartitionSpec as P

HEAD = 64
PAIR = 128
PROMPTS = 2
CHUNK = 64
SUBS = 2
EPS = 1e-05
GROUP_EPS = 0.00064
F32 = jnp.float32
BF16 = jnp.bfloat16
NN = (((1,), (0,)), ((), ()))
NT = (((1,), (1,)), ((), ()))
TN = (((0,), (0,)), ((), ()))


def split(x):
    high = x.astype(BF16)
    return high, (x - high.astype(F32)).astype(BF16)


def dot1(a, b, dims=NN):
    return lax.dot_general(a.astype(BF16), b.astype(BF16), dims, preferred_element_type=F32)


def dot3(a, b, dims=NN):
    (left,), (right,) = dims[0]
    ah, al = split(a)
    bh, bl = split(b)
    return lax.dot_general(
        jnp.concatenate([ah, al, ah], axis=left),
        jnp.concatenate([bh, bh, bl], axis=right),
        dims,
        preferred_element_type=F32,
    )


def dot_exact_right(a, b):
    ah, al = split(a)
    return lax.dot_general(
        jnp.concatenate([ah, al], axis=1),
        jnp.concatenate([b, b], axis=0),
        NN,
        preferred_element_type=F32,
    )


def head_ones():
    row = lax.broadcasted_iota(jnp.int32, (PAIR, PAIR), 0) // HEAD
    col = lax.broadcasted_iota(jnp.int32, (PAIR, PAIR), 1) // HEAD
    return (row == col).astype(BF16)


def two(x):
    lane = lax.broadcasted_iota(jnp.int32, x.shape, 1)
    zero = jnp.zeros_like(x)
    return jnp.concatenate(
        [jnp.where(lane < HEAD, x, zero), jnp.where(lane >= HEAD, x, zero)], axis=0
    )


def fold(x):
    return x[:HEAD] + x[HEAD:]


def rms_rows(x, coef):
    average = jnp.mean(x, axis=1, keepdims=True)
    centred = x - average
    variance = jnp.mean(centred * centred, axis=1, keepdims=True)
    return (centred * lax.rsqrt(variance + EPS) * coef).astype(BF16).astype(F32)


def project(
    x_ref, row_ref, cont_ref, ln_ref, mix_ref, wq_ref, wk_ref, wv_ref, fn_ref, fw_ref, fo_ref,
    sn_ref, sw_ref, so_ref, gn_ref, gw_ref, gate_ref, norm_ref, blend_ref, r_ref, k_ref, v_ref,
    fl_ref, ll_ref,
):
    tokens, features = x_ref.shape
    coef = ln_ref[0:1, :]
    first = jnp.broadcast_to(row_ref[0:1, :].astype(F32), (8, features))
    norm_ref[0:8, :] = rms_rows(first, coef)
    slab = 64
    block = 512

    def normalise(i, carry):
        rows = pl.ds(pl.multiple_of(i * slab, slab), slab)
        norm_ref[pl.ds(pl.multiple_of(8 + i * slab, 8), slab), :] = rms_rows(
            x_ref[rows, :].astype(F32), coef
        )
        return carry

    lax.fori_loop(0, tokens // slab, normalise, 0)
    for i in range(tokens // slab):
        cont = cont_ref[i * slab : (i + 1) * slab, 0:1] > 0.5
        for f in range(features // block):
            cols = slice(f * block, (f + 1) * block)
            here = norm_ref[8 + i * slab : 8 + (i + 1) * slab, cols]
            past = norm_ref[7 + i * slab : 7 + (i + 1) * slab, cols]
            gap = jnp.where(cont, past, 0.0) - here
            for w in range(6):
                blend_ref[w, i * slab : (i + 1) * slab, cols] = (
                    here + gap * mix_ref[w : w + 1, cols]
                ).astype(BF16)

    def mm(left, right):
        return jnp.dot(left, right, preferred_element_type=F32)

    r_ref[...] = mm(blend_ref[0], wq_ref[...])
    k_ref[...] = mm(blend_ref[2], wk_ref[...])
    v_ref[...] = mm(blend_ref[3], wv_ref[...])
    hidden = jnp.tanh(mm(blend_ref[1], fn_ref[...])).astype(BF16)
    fl_ref[...] = fo_ref[0:1, :] + mm(hidden, fw_ref[...])
    hidden = mm(blend_ref[4], sn_ref[...]).astype(BF16)
    ll_ref[...] = so_ref[0:1, :] + mm(hidden, sw_ref[...])
    hidden = jax.nn.sigmoid(mm(blend_ref[5], gn_ref[...])).astype(BF16)
    gate_ref[...] = mm(hidden, gw_ref[...])


def chunk_kernel(
    scal_ref, x_ref, row_ref, cont_ref, ln_ref, mix_ref, wq_ref, wk_ref, wv_ref, fn_ref, fw_ref,
    fo_ref, sn_ref, sw_ref, so_ref, gn_ref, gw_ref, er_ref, fr_ref, rw_ref, epc_ref, epr_ref,
    y_ref, z_ref, bonus_ref, a_ref, b_ref, maps_ref, gate_ref,
    run_ref, norm_ref, blend_ref, rs_ref, ks_ref, vs_ref, fl_ref, ll_ref,
):
    step = pl.program_id(0)
    last_step = pl.num_programs(0) - 1
    pairs = rs_ref.shape[1] // PAIR

    row = lax.broadcasted_iota(jnp.int32, (PAIR, PAIR), 0)
    col = lax.broadcasted_iota(jnp.int32, (PAIR, PAIR), 1)
    eye = (row == col).astype(F32)

    @pl.when(step == 0)
    def _():
        project(
            x_ref, row_ref, cont_ref, ln_ref, mix_ref, wq_ref, wk_ref, wv_ref, fn_ref, fw_ref,
            fo_ref, sn_ref, sw_ref, so_ref, gn_ref, gw_ref, gate_ref, norm_ref, blend_ref,
            rs_ref, ks_ref, vs_ref, fl_ref, ll_ref,
        )
        maps_ref[...] = jnp.zeros_like(maps_ref)
        for p in range(pairs):
            run_ref[p] = jnp.concatenate([eye, jnp.zeros_like(eye)], axis=0)

    ones = head_ones()
    tri = (
        lax.broadcasted_iota(jnp.int32, (CHUNK, CHUNK), 0)
        >= lax.broadcasted_iota(jnp.int32, (CHUNK, CHUNK), 1)
    ).astype(F32)
    sides = [slice(p * PAIR, (p + 1) * PAIR) for p in range(pairs)]
    items = []
    for sub in range(SUBS):
        c = step * SUBS + sub
        rows = pl.ds(pl.multiple_of(c * CHUNK, CHUNK), CHUNK)
        here = slice(sub * CHUNK, (sub + 1) * CHUNK)
        e_in, e_last = scal_ref[c, 0], scal_ref[c, 1]
        epc = epc_ref[here, :]
        epc2 = jnp.concatenate([epc, epc], axis=0)
        epr = epr_ref[sub, 0:1, :]
        same = (row // HEAD == col // HEAD) & (epc2 == epr)
        strict = same & (row > col)
        diag = same & (row >= col)
        from_start = (epc2 == e_in).astype(F32)
        chosen = (epc2 == e_last).astype(F32)
        keep = jnp.where(e_last == e_in, 1.0, 0.0).astype(F32)
        lw_all = -0.6065306597126334 * jax.nn.sigmoid(fl_ref[rows, :])
        lt_all = jnp.dot(tri, lw_all, precision=lax.Precision.HIGHEST, preferred_element_type=F32)
        learn_all = jax.nn.sigmoid(ll_ref[rows, :])
        for p, s in enumerate(sides):
            lw, lt, learn = lw_all[:, s], lt_all[:, s], learn_all[:, s]
            k, r, v = ks_ref[rows, s], rs_ref[rows, s], vs_ref[rows, s]
            kk = k * er_ref[0:1, s]
            n = kk * lax.rsqrt(dot_exact_right(kk * kk, ones) + 1e-06)
            w = k * (1.0 + (learn - 1.0) * fr_ref[0:1, s])
            inv = jnp.exp(-lt)
            beta = n * learn * inv
            key = w * inv
            bonus_ref[here, s] = dot_exact_right(r * w * rw_ref[0:1, s], ones) * v
            qa2, q2 = two(-n * jnp.exp(lt - lw)), two(r * jnp.exp(lt))
            right = jnp.concatenate([beta, beta, key, key], axis=0)
            mixed = dot3(qa2, right, NT)
            read = dot1(q2, right, NT)
            items.append(
                dict(
                    c=c, sub=sub, p=p, s=s, here=here, lt=lt, epc2=epc2, e_in=e_in,
                    start=from_start, chosen=chosen, keep=keep,
                    qa=qa2, q=q2, beta=two(beta), key=two(key), v=two(v),
                    mix=jnp.where(strict, mixed[:, :PAIR], 0.0),
                    mix_key=jnp.where(strict, mixed[:, PAIR:], 0.0),
                    read_beta=jnp.where(diag, read[:, :PAIR], 0.0),
                    read_key=jnp.where(diag, read[:, PAIR:], 0.0),
                )
            )
    mixes = [i["mix"] for i in items]
    inverses = [eye + jnp.where(row // 2 == col // 2, m, 0.0) for m in mixes]
    b = 2
    while b < CHUNK:
        off = (row // (2 * b) == col // (2 * b)) & (row // b != col // b)
        inner = [dot1(jnp.where(off, m, 0.0), x) for m, x in zip(mixes, inverses)]
        inverses = [x + dot1(x, i) for x, i in zip(inverses, inner)]
        b *= 2
    rests = [eye - x + dot3(m, x) for m, x in zip(mixes, inverses)]
    inverses = [x + dot1(x, i) for x, i in zip(inverses, rests)]
    kvs = [dot3(i["mix_key"], i["v"]) for i in items]
    uws = [
        dot3(x, jnp.concatenate([kv, i["qa"] * i["start"]], axis=1))
        for x, kv, i in zip(inverses, kvs, items)
    ]
    for uw, i in zip(uws, items):
        rb = dot1(i["read_beta"], uw)
        rk = dot1(i["read_key"], i["v"])
        z_ref[i["here"], i["s"]] = fold(rb[:, :PAIR] + rk)
        y_ref[i["here"], i["s"]] = fold(rb[:, PAIR:] + i["q"] * i["start"])

    def maps(uw, i, weight, growth, kept):
        bw = i["beta"] * (weight * growth)
        kw = i["key"] * (weight * growth)
        both = dot3(uw, bw, TN)
        extra = dot3(i["v"], kw, TN)
        return both[PAIR:] + eye * (growth * kept), both[:PAIR] + extra

    pieces = [
        maps(uw, i, i["chosen"], jnp.exp(i["lt"][CHUNK - 1 : CHUNK]), i["keep"])
        for uw, i in zip(uws, items)
    ]
    for uw, i, (a_map, b_map) in zip(uws, items, pieces):
        p, c, sub = i["p"], i["c"], i["sub"]
        earlier = run_ref[p]
        a_ref[sub, p] = a_map
        b_ref[sub, p] = b_map
        later = dot3(earlier, a_map)
        run_ref[p] = later + jnp.concatenate([jnp.zeros_like(b_map), b_map], axis=0)

        @pl.when(scal_ref[c, 2] == 1)
        def _(uw=uw, i=i, p=p, c=c, earlier=earlier):
            moment, e_end = scal_ref[c, 3], scal_ref[c, 4]
            place = jnp.where(row < CHUNK, row, row - CHUNK)
            here = ((i["epc2"] == e_end) & (place <= moment)).astype(F32)
            pick = lax.broadcasted_iota(jnp.int32, (CHUNK, PAIR), 0) == moment
            grow = jnp.exp(jnp.sum(jnp.where(pick, i["lt"], 0.0), axis=0, keepdims=True))
            kept = jnp.where(e_end == i["e_in"], 1.0, 0.0).astype(F32)
            a_end, b_end = maps(uw, i, here, grow, kept)
            ended = dot3(earlier, a_end)
            maps_ref[0, p] = fold(ended[:PAIR]).astype(BF16)
            maps_ref[2, p] = fold(ended[PAIR:] + b_end).astype(BF16)

    @pl.when(step == last_step)
    def _():
        for p in range(pairs):
            maps_ref[1, p] = fold(run_ref[p, PAIR:]).astype(BF16)

        @pl.when(scal_ref[0, 5] == 0)
        def _():
            for p in range(pairs):
                maps_ref[0, p] = fold(run_ref[p, :PAIR]).astype(BF16)


def read_kernel(
    scal_ref, all_ref, y_ref, z_ref, bonus_ref, gate_ref, gain_ref, a_ref, b_ref,
    vis_ref, final_ref, state_ref, mine_ref,
):
    c = pl.program_id(0)
    pairs = y_ref.shape[1] // PAIR
    count = all_ref.shape[0]
    position = scal_ref[0]

    @pl.when(c == 0)
    def _():
        final_ref[...] = jnp.zeros_like(final_ref)
        state_ref[...] = jnp.zeros_like(state_ref)

        def hop(d, carry):
            @pl.when(d == position)
            def _():
                mine_ref[...] = state_ref[...]

            holds = (d == scal_ref[1]) | (d == scal_ref[2])
            owner = jnp.where(d == scal_ref[1], scal_ref[3], scal_ref[4])

            for p in range(pairs):
                state = state_ref[p]
                high, low = split(state)
                a_map = two(all_ref[d, 0, p].astype(F32)).astype(BF16)
                moved = lax.dot_general(high, a_map, NN, preferred_element_type=F32)
                moved = moved + lax.dot_general(low, a_map, NN, preferred_element_type=F32)

                @pl.when(holds & (owner == position))
                def _():
                    final_ref[p] = fold(moved) + all_ref[d, 2, p].astype(F32)

                local = two(all_ref[d, 1, p].astype(F32))
                state_ref[p] = jnp.where(holds, 0.0, moved) + local
            return carry

        lax.fori_loop(0, count, hop, 0)

    ones = head_ones()
    for p in range(pairs):
        s = slice(p * PAIR, (p + 1) * PAIR)
        state = mine_ref[p]
        out = fold(dot1(two(y_ref[:, s]), state, NT)) + z_ref[:, s]
        mine_ref[p] = dot3(state, a_ref[0, p]) + b_ref[0, p]
        centre = out - dot_exact_right(out, ones) * (1.0 / HEAD)
        spread = dot_exact_right(centre * centre, ones) * (1.0 / HEAD)
        normed = centre * lax.rsqrt(spread + GROUP_EPS) * gain_ref[0:1, s]
        vis_ref[:, s] = ((normed + bonus_ref[:, s]) * gate_ref[:, s]).astype(BF16)


def from_behind(array, axis, by):
    length = lax.axis_size(axis)
    pairs = [(i, i + by) for i in range(length) if 0 <= i + by < length]
    return lax.ppermute(array, axis, pairs)


def on_device(
    layer_activation,
    sequence_label,
    sequence_extents,
    destination_slots,
    entry_layernorm_coef,
    lagged_blend_coefs,
    query_matrix,
    lookup_matrix,
    content_matrix,
    readout_matrix,
    forgetting_narrow_matrix,
    forgetting_widen_matrix,
    forgetting_offset,
    stepsize_narrow_matrix,
    stepsize_widen_matrix,
    stepsize_offset,
    gating_narrow_matrix,
    gating_widen_matrix,
    erasure_lookup_coef,
    lookup_step_fraction,
    diagonal_reward_coef,
    group_layernorm_coef,
):
    tokens = layer_activation.shape[0]
    width = query_matrix.shape[1]
    pairs = width // PAIR
    chunks = tokens // CHUNK
    position = lax.axis_index("seq")
    column = lax.axis_index("tp")
    n_seq = lax.axis_size("seq")
    gathered = lax.all_gather(layer_activation, "tp", axis=1, tiled=True)
    arrived = from_behind(gathered[-1:], "seq", 1)
    bounds = jnp.cumsum(sequence_extents)
    first_token = position * tokens
    before = first_token - 1
    segment_before = (before >= bounds[0]).astype(jnp.int32) + (before >= bounds[1]).astype(
        jnp.int32
    )
    joined = (segment_before == sequence_label[0]) & (position > 0)
    continues = jnp.concatenate([joined[None], sequence_label[1:] == sequence_label[:-1]])
    ends = bounds - 1
    holders = ends // tokens
    epochs = sequence_label
    before_first = jnp.where(position > 0, segment_before, -1)
    grouped = epochs.reshape(chunks, CHUNK)
    e_last = grouped[:, -1]
    e_in = jnp.concatenate([before_first[None], e_last[:-1]])
    starts = first_token + jnp.arange(chunks, dtype=jnp.int32) * CHUNK
    offsets = ends[None, :] - starts[:, None]
    within = (offsets >= 0) & (offsets < CHUNK)
    inside = jnp.any(within, axis=1).astype(jnp.int32)
    moment = jnp.sum(jnp.where(within, offsets, 0), axis=1)
    e_end = jnp.sum(jnp.where(within, jnp.arange(PROMPTS, dtype=jnp.int32)[None], 0), axis=1)
    device_ends = jnp.broadcast_to(jnp.any(holders == position).astype(jnp.int32), (chunks,))
    scalars = jnp.stack([e_in, e_last, inside, moment, e_end, device_ends], axis=1)
    ep_cols = jnp.broadcast_to(epochs[:, None], (tokens, PAIR))
    ep_rows = jnp.broadcast_to(
        jnp.concatenate([grouped, grouped], axis=1)[:, None, :], (chunks, 8, PAIR)
    )

    rows_per_step = CHUNK * SUBS

    def wide():
        return pl.BlockSpec((rows_per_step, width), lambda c: (c, 0))

    def tall():
        return pl.BlockSpec((CHUNK, width), lambda c: (c, 0))

    def coef():
        return pl.BlockSpec((1, width), lambda c: (0, 0))

    def whole(array):
        return pl.BlockSpec(array.shape, lambda c: (0,) * array.ndim, pipeline_mode=pl.Buffered(1))

    def mats(many):
        return pl.BlockSpec((many, pairs, PAIR, PAIR), lambda c: (c, 0, 0, 0))

    smem = pl.BlockSpec(memory_space=pltpu.SMEM)
    big = jax.ShapeDtypeStruct((tokens, width), F32)
    mat = jax.ShapeDtypeStruct((chunks, pairs, PAIR, PAIR), F32)
    fixed = [
        gathered,
        arrived,
        jnp.broadcast_to(continues.astype(F32)[:, None], (tokens, PAIR)),
        entry_layernorm_coef[None],
        lagged_blend_coefs,
        query_matrix,
        lookup_matrix,
        content_matrix,
        forgetting_narrow_matrix,
        forgetting_widen_matrix,
        forgetting_offset[None],
        stepsize_narrow_matrix,
        stepsize_widen_matrix,
        stepsize_offset[None],
        gating_narrow_matrix,
        gating_widen_matrix,
        erasure_lookup_coef[None],
        lookup_step_fraction[None],
        diagonal_reward_coef[None],
    ]
    features = gathered.shape[1]
    y, z, bonus, a_maps, b_maps, maps, gating_signal = pl.pallas_call(
        chunk_kernel,
        grid=(chunks // SUBS,),
        in_specs=[smem]
        + [whole(array) for array in fixed]
        + [
            pl.BlockSpec((rows_per_step, PAIR), lambda c: (c, 0)),
            pl.BlockSpec((SUBS, 8, PAIR), lambda c: (c, 0, 0)),
        ],
        out_specs=[
            wide(),
            wide(),
            wide(),
            mats(SUBS),
            mats(SUBS),
            pl.BlockSpec((3, pairs, HEAD, PAIR), lambda c: (0, 0, 0, 0)),
            pl.BlockSpec((tokens, width), lambda c: (0, 0)),
        ],
        out_shape=[
            big,
            big,
            big,
            mat,
            mat,
            jax.ShapeDtypeStruct((3, pairs, HEAD, PAIR), BF16),
            big,
        ],
        scratch_shapes=[
            pltpu.VMEM((pairs, 2 * PAIR, PAIR), F32),
            pltpu.VMEM((tokens + 8, features), F32),
            pltpu.VMEM((6, tokens, features), BF16),
        ]
        + [pltpu.VMEM((tokens, width), F32)] * 5,
        compiler_params=pltpu.CompilerParams(vmem_limit_bytes=56 << 20),
    )(scalars, *fixed, ep_cols, ep_rows)

    local_end = jnp.clip(jnp.max(jnp.where(holders == position, ends - first_token, 0)), 0, tokens - 1)
    row_raw = lax.dynamic_slice(gathered, (local_end, 0), (1, features)).astype(F32)
    row_norm = rms_rows(row_raw, entry_layernorm_coef).astype(BF16)
    row_end = lax.dynamic_slice(row_norm, (0, column * width), (1, width))
    sent = jnp.concatenate(
        [
            maps.reshape(3 * pairs * HEAD, PAIR),
            jnp.pad(row_end.reshape(pairs, PAIR), ((0, 16 - pairs), (0, 0))),
        ],
        axis=0,
    )
    everyone = lax.all_gather(sent, "seq", axis=0, tiled=False)
    all_maps = everyone[:, : 3 * pairs * HEAD].reshape(n_seq, 3, pairs, HEAD, PAIR)
    rows = everyone[:, 3 * pairs * HEAD : 3 * pairs * HEAD + pairs].reshape(n_seq, width)

    facts = jnp.concatenate([position[None], holders, destination_slots]).astype(jnp.int32)
    visible, final_fold = pl.pallas_call(
        read_kernel,
        grid=(chunks,),
        in_specs=[
            smem,
            pl.BlockSpec((n_seq, 3, pairs, HEAD, PAIR), lambda c: (0, 0, 0, 0, 0), pipeline_mode=pl.Buffered(1)),
            tall(),
            tall(),
            tall(),
            tall(),
            coef(),
            mats(1),
            mats(1),
        ],
        out_specs=[tall(), pl.BlockSpec((pairs, HEAD, PAIR), lambda c: (0, 0, 0))],
        out_shape=[
            jax.ShapeDtypeStruct((tokens, width), BF16),
            jax.ShapeDtypeStruct((pairs, HEAD, PAIR), F32),
        ],
        scratch_shapes=[pltpu.VMEM((pairs, PAIR, PAIR), F32), pltpu.VMEM((pairs, PAIR, PAIR), F32)],
        compiler_params=pltpu.CompilerParams(vmem_limit_bytes=48 << 20),
    )(facts, all_maps, y, z, bonus, gating_signal, group_layernorm_coef[None], a_maps, b_maps)

    final_states = final_fold.reshape(pairs, HEAD, 2, HEAD).transpose(0, 2, 1, 3)
    final_states = final_states.reshape(1, 2 * pairs, HEAD, HEAD)
    final_rows = jnp.zeros((1, width), BF16)
    for prompt in range(PROMPTS):
        got = lax.dynamic_slice(rows, (holders[prompt], 0), (1, width))
        final_rows = jnp.where(position == destination_slots[prompt], got, final_rows)

    partial_value = jnp.dot(visible, readout_matrix, preferred_element_type=F32)
    summed = lax.psum_scatter(
        partial_value.astype(BF16), "tp", scatter_dimension=1, tiled=True
    ).astype(F32)
    mixed = (summed + layer_activation.astype(F32)).astype(BF16)
    return (mixed, final_states, final_rows)


def solution(mesh):
    return jax.shard_map(
        on_device,
        mesh=mesh,
        in_specs=(
            P("seq", "tp"),
            P("seq"),
            P(),
            P(),
            P(),
            P(),
            P(None, "tp"),
            P(None, "tp"),
            P(None, "tp"),
            P("tp", None),
            P(),
            P(None, "tp"),
            P("tp"),
            P(),
            P(None, "tp"),
            P("tp"),
            P(),
            P(None, "tp"),
            P("tp"),
            P("tp"),
            P("tp"),
            P("tp"),
        ),
        out_specs=(P("seq", "tp"), P("seq", "tp", None, None), P("seq", "tp")),
        check_vma=False,
    )
```

```python
import jax
import jax.numpy as jnp
from jax import lax
from jax.experimental import pallas as pl
from jax.experimental.pallas import tpu as pltpu
from jax.sharding import PartitionSpec as P

HEAD = 64
PAIR = 128
PROMPTS = 2
CHUNK = 64
SUBS = 2
EPS = 1e-05
GROUP_EPS = 0.00064
F32 = jnp.float32
BF16 = jnp.bfloat16
NN = (((1,), (0,)), ((), ()))
NT = (((1,), (1,)), ((), ()))
TN = (((0,), (0,)), ((), ()))


def split(x):
    high = x.astype(BF16)
    return high, (x - high.astype(F32)).astype(BF16)


def dot1(a, b, dims=NN):
    return lax.dot_general(a.astype(BF16), b.astype(BF16), dims, preferred_element_type=F32)


def dot3(a, b, dims=NN):
    (left,), (right,) = dims[0]
    ah, al = split(a)
    bh, bl = split(b)
    return lax.dot_general(
        jnp.concatenate([ah, al, ah], axis=left),
        jnp.concatenate([bh, bh, bl], axis=right),
        dims,
        preferred_element_type=F32,
    )


def dot_exact_right(a, b):
    ah, al = split(a)
    return lax.dot_general(
        jnp.concatenate([ah, al], axis=1),
        jnp.concatenate([b, b], axis=0),
        NN,
        preferred_element_type=F32,
    )


def head_ones():
    row = lax.broadcasted_iota(jnp.int32, (PAIR, PAIR), 0) // HEAD
    col = lax.broadcasted_iota(jnp.int32, (PAIR, PAIR), 1) // HEAD
    return (row == col).astype(BF16)


def two(x):
    lane = lax.broadcasted_iota(jnp.int32, x.shape, 1)
    zero = jnp.zeros_like(x)
    return jnp.concatenate(
        [jnp.where(lane < HEAD, x, zero), jnp.where(lane >= HEAD, x, zero)], axis=0
    )


def fold(x):
    return x[:HEAD] + x[HEAD:]


def rms_rows(x, coef):
    average = jnp.mean(x, axis=1, keepdims=True)
    centred = x - average
    variance = jnp.mean(centred * centred, axis=1, keepdims=True)
    return (centred * lax.rsqrt(variance + EPS) * coef).astype(BF16).astype(F32)


def project(
    x_ref, row_ref, cont_ref, ln_ref, mix_ref, wq_ref, wk_ref, wv_ref, fn_ref, fw_ref, fo_ref,
    sn_ref, sw_ref, so_ref, gn_ref, gw_ref, gate_ref, norm_ref, blend_ref, r_ref, k_ref, v_ref,
    fl_ref, ll_ref,
):
    tokens, features = x_ref.shape
    coef = ln_ref[0:1, :]
    first = jnp.broadcast_to(row_ref[0:1, :].astype(F32), (8, features))
    norm_ref[0:8, :] = rms_rows(first, coef)
    slab = 64
    block = 512

    def normalise(i, carry):
        rows = pl.ds(pl.multiple_of(i * slab, slab), slab)
        norm_ref[pl.ds(pl.multiple_of(8 + i * slab, 8), slab), :] = rms_rows(
            x_ref[rows, :].astype(F32), coef
        )
        return carry

    lax.fori_loop(0, tokens // slab, normalise, 0)
    for i in range(tokens // slab):
        cont = cont_ref[i * slab : (i + 1) * slab, 0:1] > 0.5
        for f in range(features // block):
            cols = slice(f * block, (f + 1) * block)
            here = norm_ref[8 + i * slab : 8 + (i + 1) * slab, cols]
            past = norm_ref[7 + i * slab : 7 + (i + 1) * slab, cols]
            gap = jnp.where(cont, past, 0.0) - here
            for w in range(6):
                blend_ref[w, i * slab : (i + 1) * slab, cols] = (
                    here + gap * mix_ref[w : w + 1, cols]
                ).astype(BF16)

    def mm(left, right):
        return jnp.dot(left, right, preferred_element_type=F32)

    r_ref[...] = mm(blend_ref[0], wq_ref[...])
    k_ref[...] = mm(blend_ref[2], wk_ref[...])
    v_ref[...] = mm(blend_ref[3], wv_ref[...])
    hidden = jnp.tanh(mm(blend_ref[1], fn_ref[...])).astype(BF16)
    fl_ref[...] = fo_ref[0:1, :] + mm(hidden, fw_ref[...])
    hidden = mm(blend_ref[4], sn_ref[...]).astype(BF16)
    ll_ref[...] = so_ref[0:1, :] + mm(hidden, sw_ref[...])
    hidden = jax.nn.sigmoid(mm(blend_ref[5], gn_ref[...])).astype(BF16)
    gate_ref[...] = mm(hidden, gw_ref[...])


def chunk_kernel(
    scal_ref, x_ref, row_ref, cont_ref, ln_ref, mix_ref, wq_ref, wk_ref, wv_ref, fn_ref, fw_ref,
    fo_ref, sn_ref, sw_ref, so_ref, gn_ref, gw_ref, er_ref, fr_ref, rw_ref, epc_ref, epr_ref,
    y_ref, z_ref, bonus_ref, a_ref, b_ref, maps_ref, gate_ref,
    run_ref, norm_ref, blend_ref, rs_ref, ks_ref, vs_ref, fl_ref, ll_ref,
):
    step = pl.program_id(0)
    last_step = pl.num_programs(0) - 1
    pairs = rs_ref.shape[1] // PAIR

    row = lax.broadcasted_iota(jnp.int32, (PAIR, PAIR), 0)
    col = lax.broadcasted_iota(jnp.int32, (PAIR, PAIR), 1)
    eye = (row == col).astype(F32)

    @pl.when(step == 0)
    def _():
        project(
            x_ref, row_ref, cont_ref, ln_ref, mix_ref, wq_ref, wk_ref, wv_ref, fn_ref, fw_ref,
            fo_ref, sn_ref, sw_ref, so_ref, gn_ref, gw_ref, gate_ref, norm_ref, blend_ref,
            rs_ref, ks_ref, vs_ref, fl_ref, ll_ref,
        )
        maps_ref[...] = jnp.zeros_like(maps_ref)
        for p in range(pairs):
            run_ref[p] = jnp.concatenate([eye, jnp.zeros_like(eye)], axis=0)

    ones = head_ones()
    tri = (
        lax.broadcasted_iota(jnp.int32, (CHUNK, CHUNK), 0)
        >= lax.broadcasted_iota(jnp.int32, (CHUNK, CHUNK), 1)
    ).astype(F32)
    sides = [slice(p * PAIR, (p + 1) * PAIR) for p in range(pairs)]
    items = []
    for sub in range(SUBS):
        c = step * SUBS + sub
        rows = pl.ds(pl.multiple_of(c * CHUNK, CHUNK), CHUNK)
        here = slice(sub * CHUNK, (sub + 1) * CHUNK)
        e_in, e_last = scal_ref[c, 0], scal_ref[c, 1]
        epc = epc_ref[here, :]
        epc2 = jnp.concatenate([epc, epc], axis=0)
        epr = epr_ref[sub, 0:1, :]
        same = (row // HEAD == col // HEAD) & (epc2 == epr)
        strict = same & (row > col)
        diag = same & (row >= col)
        from_start = (epc2 == e_in).astype(F32)
        chosen = (epc2 == e_last).astype(F32)
        keep = jnp.where(e_last == e_in, 1.0, 0.0).astype(F32)
        lw_all = -0.6065306597126334 * jax.nn.sigmoid(fl_ref[rows, :])
        lt_all = jnp.dot(tri, lw_all, precision=lax.Precision.HIGHEST, preferred_element_type=F32)
        learn_all = jax.nn.sigmoid(ll_ref[rows, :])
        for p, s in enumerate(sides):
            lw, lt, learn = lw_all[:, s], lt_all[:, s], learn_all[:, s]
            k, r, v = ks_ref[rows, s], rs_ref[rows, s], vs_ref[rows, s]
            kk = k * er_ref[0:1, s]
            n = kk * lax.rsqrt(dot_exact_right(kk * kk, ones) + 1e-06)
            w = k * (1.0 + (learn - 1.0) * fr_ref[0:1, s])
            inv = jnp.exp(-lt)
            beta = n * learn * inv
            key = w * inv
            bonus_ref[here, s] = dot_exact_right(r * w * rw_ref[0:1, s], ones) * v
            qa2, q2 = two(-n * jnp.exp(lt - lw)), two(r * jnp.exp(lt))
            right = jnp.concatenate([beta, beta, key, key], axis=0)
            mixed = dot3(qa2, right, NT)
            read = dot1(q2, right, NT)
            items.append(
                dict(
                    c=c, sub=sub, p=p, s=s, here=here, lt=lt, epc2=epc2, e_in=e_in,
                    start=from_start, chosen=chosen, keep=keep,
                    qa=qa2, q=q2, beta=two(beta), key=two(key), v=two(v),
                    mix=jnp.where(strict, mixed[:, :PAIR], 0.0),
                    mix_key=jnp.where(strict, mixed[:, PAIR:], 0.0),
                    read_beta=jnp.where(diag, read[:, :PAIR], 0.0),
                    read_key=jnp.where(diag, read[:, PAIR:], 0.0),
                )
            )
    mixes = [i["mix"] for i in items]
    inverses = [eye + jnp.where(row // 2 == col // 2, m, 0.0) for m in mixes]
    b = 2
    while b < CHUNK:
        off = (row // (2 * b) == col // (2 * b)) & (row // b != col // b)
        inner = [dot1(jnp.where(off, m, 0.0), x) for m, x in zip(mixes, inverses)]
        inverses = [x + dot1(x, i) for x, i in zip(inverses, inner)]
        b *= 2
    rests = [eye - x + dot3(m, x) for m, x in zip(mixes, inverses)]
    inverses = [x + dot1(x, i) for x, i in zip(inverses, rests)]
    kvs = [dot3(i["mix_key"], i["v"]) for i in items]
    uws = [
        dot3(x, jnp.concatenate([kv, i["qa"] * i["start"]], axis=1))
        for x, kv, i in zip(inverses, kvs, items)
    ]
    for uw, i in zip(uws, items):
        rb = dot1(i["read_beta"], uw)
        rk = dot1(i["read_key"], i["v"])
        z_ref[i["here"], i["s"]] = fold(rb[:, :PAIR] + rk)
        y_ref[i["here"], i["s"]] = fold(rb[:, PAIR:] + i["q"] * i["start"])

    def maps(uw, i, weight, growth, kept):
        bw = i["beta"] * (weight * growth)
        kw = i["key"] * (weight * growth)
        both = dot3(uw, bw, TN)
        extra = dot3(i["v"], kw, TN)
        return both[PAIR:] + eye * (growth * kept), both[:PAIR] + extra

    pieces = [
        maps(uw, i, i["chosen"], jnp.exp(i["lt"][CHUNK - 1 : CHUNK]), i["keep"])
        for uw, i in zip(uws, items)
    ]
    for uw, i, (a_map, b_map) in zip(uws, items, pieces):
        p, c, sub = i["p"], i["c"], i["sub"]
        earlier = run_ref[p]
        a_ref[sub, p] = a_map
        b_ref[sub, p] = b_map
        later = dot3(earlier, a_map)
        run_ref[p] = later + jnp.concatenate([jnp.zeros_like(b_map), b_map], axis=0)

        @pl.when(scal_ref[c, 2] == 1)
        def _(uw=uw, i=i, p=p, c=c, earlier=earlier):
            moment, e_end = scal_ref[c, 3], scal_ref[c, 4]
            place = jnp.where(row < CHUNK, row, row - CHUNK)
            here = ((i["epc2"] == e_end) & (place <= moment)).astype(F32)
            pick = lax.broadcasted_iota(jnp.int32, (CHUNK, PAIR), 0) == moment
            grow = jnp.exp(jnp.sum(jnp.where(pick, i["lt"], 0.0), axis=0, keepdims=True))
            kept = jnp.where(e_end == i["e_in"], 1.0, 0.0).astype(F32)
            a_end, b_end = maps(uw, i, here, grow, kept)
            ended = dot3(earlier, a_end)
            maps_ref[3, p] = fold(ended[:PAIR])
            maps_ref[2, p] = fold(ended[PAIR:] + b_end)

    @pl.when(step == last_step)
    def _():
        for p in range(pairs):
            maps_ref[0, p] = fold(run_ref[p, :PAIR])
            maps_ref[1, p] = fold(run_ref[p, PAIR:])


def chain_kernel(maps_ref, state_ref, end_ref, going, coming, send_sem, recv_sem):
    me = lax.axis_index("seq")
    n = lax.axis_size("seq")
    pairs = maps_ref.shape[1]
    right = lax.rem(me + 1, n)
    left = lax.rem(me + n - 1, n)
    barrier = pltpu.get_barrier_semaphore()

    @pl.when(me > 0)
    def _():
        pl.semaphore_signal(
            barrier, inc=1, device_id={"seq": left}, device_id_type=pl.DeviceIdType.MESH
        )

    @pl.when(me < n - 1)
    def _():
        pl.semaphore_signal(
            barrier, inc=1, device_id={"seq": right}, device_id_type=pl.DeviceIdType.MESH
        )

    @pl.when(me == 0)
    def _():
        coming[...] = jnp.zeros_like(coming)

    def factor(which, p):
        return jnp.concatenate(split(two(maps_ref[which, p])), axis=0)

    factors = [factor(0, p) for p in range(pairs)]

    @pl.when((me > 0) & (me < n - 1))
    def _():
        pl.semaphore_wait(barrier, 2)

    @pl.when((me == 0) | (me == n - 1))
    def _():
        pl.semaphore_wait(barrier, 1)

    def advance(p, right_side, which):
        state = two(coming[p].astype(F32)).astype(BF16)
        moved = lax.dot_general(
            jnp.concatenate([state, state], axis=1), right_side, NN, preferred_element_type=F32
        )
        return (fold(moved) + maps_ref[which, p]).astype(BF16)

    copies = [
        pltpu.make_async_remote_copy(
            src_ref=going.at[p],
            dst_ref=coming.at[p],
            send_sem=send_sem.at[p],
            recv_sem=recv_sem.at[p],
            device_id={"seq": right},
            device_id_type=pl.DeviceIdType.MESH,
        )
        for p in range(pairs)
    ]
    for p in range(pairs):

        @pl.when(me > 0)
        def _(p=p):
            copies[p].wait_recv()

        going[p] = advance(p, factors[p], 1)

        @pl.when(me < n - 1)
        def _(p=p):
            copies[p].start()

    for p in range(pairs):
        state_ref[p] = coming[p].astype(F32)
        end_ref[p] = advance(p, factor(3, p), 2)

    @pl.when(me < n - 1)
    def _():
        for p in range(pairs):
            copies[p].wait_send()


def read_kernel(
    state_ref, y_ref, z_ref, bonus_ref, gate_ref, gain_ref, a_ref, b_ref, vis_ref, mine_ref
):
    pairs = y_ref.shape[1] // PAIR

    @pl.when(pl.program_id(0) == 0)
    def _():
        for p in range(pairs):
            mine_ref[p] = two(state_ref[p])

    ones = head_ones()
    for p in range(pairs):
        s = slice(p * PAIR, (p + 1) * PAIR)
        state = mine_ref[p]
        out = fold(dot1(two(y_ref[:, s]), state, NT)) + z_ref[:, s]
        mine_ref[p] = dot3(state, a_ref[0, p]) + b_ref[0, p]
        centre = out - dot_exact_right(out, ones) * (1.0 / HEAD)
        spread = dot_exact_right(centre * centre, ones) * (1.0 / HEAD)
        normed = centre * lax.rsqrt(spread + GROUP_EPS) * gain_ref[0:1, s]
        vis_ref[:, s] = ((normed + bonus_ref[:, s]) * gate_ref[:, s]).astype(BF16)


def from_behind(array, axis, by):
    length = lax.axis_size(axis)
    pairs = [(i, i + by) for i in range(length) if 0 <= i + by < length]
    return lax.ppermute(array, axis, pairs)


def on_device(
    layer_activation,
    sequence_label,
    sequence_extents,
    destination_slots,
    entry_layernorm_coef,
    lagged_blend_coefs,
    query_matrix,
    lookup_matrix,
    content_matrix,
    readout_matrix,
    forgetting_narrow_matrix,
    forgetting_widen_matrix,
    forgetting_offset,
    stepsize_narrow_matrix,
    stepsize_widen_matrix,
    stepsize_offset,
    gating_narrow_matrix,
    gating_widen_matrix,
    erasure_lookup_coef,
    lookup_step_fraction,
    diagonal_reward_coef,
    group_layernorm_coef,
):
    tokens = layer_activation.shape[0]
    width = query_matrix.shape[1]
    pairs = width // PAIR
    chunks = tokens // CHUNK
    position = lax.axis_index("seq")
    column = lax.axis_index("tp")
    gathered = lax.all_gather(layer_activation, "tp", axis=1, tiled=True)
    arrived = from_behind(gathered[-1:], "seq", 1)
    bounds = jnp.cumsum(sequence_extents)
    first_token = position * tokens
    before = first_token - 1
    segment_before = (before >= bounds[0]).astype(jnp.int32) + (before >= bounds[1]).astype(
        jnp.int32
    )
    joined = (segment_before == sequence_label[0]) & (position > 0)
    continues = jnp.concatenate([joined[None], sequence_label[1:] == sequence_label[:-1]])
    ends = bounds - 1
    holders = ends // tokens
    epochs = sequence_label
    before_first = jnp.where(position > 0, segment_before, -1)
    grouped = epochs.reshape(chunks, CHUNK)
    e_last = grouped[:, -1]
    e_in = jnp.concatenate([before_first[None], e_last[:-1]])
    starts = first_token + jnp.arange(chunks, dtype=jnp.int32) * CHUNK
    offsets = ends[None, :] - starts[:, None]
    within = (offsets >= 0) & (offsets < CHUNK)
    inside = jnp.any(within, axis=1).astype(jnp.int32)
    moment = jnp.sum(jnp.where(within, offsets, 0), axis=1)
    e_end = jnp.sum(jnp.where(within, jnp.arange(PROMPTS, dtype=jnp.int32)[None], 0), axis=1)
    device_ends = jnp.broadcast_to(jnp.any(holders == position).astype(jnp.int32), (chunks,))
    scalars = jnp.stack([e_in, e_last, inside, moment, e_end, device_ends], axis=1)
    ep_cols = jnp.broadcast_to(epochs[:, None], (tokens, PAIR))
    ep_rows = jnp.broadcast_to(
        jnp.concatenate([grouped, grouped], axis=1)[:, None, :], (chunks, 8, PAIR)
    )

    rows_per_step = CHUNK * SUBS

    def wide():
        return pl.BlockSpec((rows_per_step, width), lambda c: (c, 0))

    def tall():
        return pl.BlockSpec((CHUNK, width), lambda c: (c, 0))

    def coef():
        return pl.BlockSpec((1, width), lambda c: (0, 0))

    def whole(array):
        return pl.BlockSpec(array.shape, lambda c: (0,) * array.ndim, pipeline_mode=pl.Buffered(1))

    def mats(many):
        return pl.BlockSpec((many, pairs, PAIR, PAIR), lambda c: (c, 0, 0, 0))

    smem = pl.BlockSpec(memory_space=pltpu.SMEM)
    big = jax.ShapeDtypeStruct((tokens, width), F32)
    mat = jax.ShapeDtypeStruct((chunks, pairs, PAIR, PAIR), F32)
    fixed = [
        gathered,
        arrived,
        jnp.broadcast_to(continues.astype(F32)[:, None], (tokens, PAIR)),
        entry_layernorm_coef[None],
        lagged_blend_coefs,
        query_matrix,
        lookup_matrix,
        content_matrix,
        forgetting_narrow_matrix,
        forgetting_widen_matrix,
        forgetting_offset[None],
        stepsize_narrow_matrix,
        stepsize_widen_matrix,
        stepsize_offset[None],
        gating_narrow_matrix,
        gating_widen_matrix,
        erasure_lookup_coef[None],
        lookup_step_fraction[None],
        diagonal_reward_coef[None],
    ]
    features = gathered.shape[1]
    y, z, bonus, a_maps, b_maps, maps, gating_signal = pl.pallas_call(
        chunk_kernel,
        grid=(chunks // SUBS,),
        in_specs=[smem]
        + [whole(array) for array in fixed]
        + [
            pl.BlockSpec((rows_per_step, PAIR), lambda c: (c, 0)),
            pl.BlockSpec((SUBS, 8, PAIR), lambda c: (c, 0, 0)),
        ],
        out_specs=[
            wide(),
            wide(),
            wide(),
            mats(SUBS),
            mats(SUBS),
            pl.BlockSpec((4, pairs, HEAD, PAIR), lambda c: (0, 0, 0, 0)),
            pl.BlockSpec((tokens, width), lambda c: (0, 0)),
        ],
        out_shape=[
            big,
            big,
            big,
            mat,
            mat,
            jax.ShapeDtypeStruct((4, pairs, HEAD, PAIR), F32),
            big,
        ],
        scratch_shapes=[
            pltpu.VMEM((pairs, 2 * PAIR, PAIR), F32),
            pltpu.VMEM((tokens + 8, features), F32),
            pltpu.VMEM((6, tokens, features), BF16),
        ]
        + [pltpu.VMEM((tokens, width), F32)] * 5,
        compiler_params=pltpu.CompilerParams(vmem_limit_bytes=56 << 20),
    )(scalars, *fixed, ep_cols, ep_rows)

    local_end = jnp.clip(jnp.max(jnp.where(holders == position, ends - first_token, 0)), 0, tokens - 1)
    row_raw = lax.dynamic_slice(gathered, (local_end, 0), (1, features)).astype(F32)
    row_norm = rms_rows(row_raw, entry_layernorm_coef).astype(BF16)
    row_end = lax.dynamic_slice(row_norm, (0, column * width), (1, width))
    vmem = pl.BlockSpec(memory_space=pltpu.VMEM)
    state_in, end_state = pl.pallas_call(
        chain_kernel,
        in_specs=[vmem],
        out_specs=[vmem, vmem],
        out_shape=[
            jax.ShapeDtypeStruct((pairs, HEAD, PAIR), F32),
            jax.ShapeDtypeStruct((pairs, HEAD, PAIR), BF16),
        ],
        scratch_shapes=[
            pltpu.VMEM((pairs, HEAD, PAIR), BF16),
            pltpu.VMEM((pairs, HEAD, PAIR), BF16),
            pltpu.SemaphoreType.DMA((pairs,)),
            pltpu.SemaphoreType.DMA((pairs,)),
        ],
        compiler_params=pltpu.CompilerParams(collective_id=0, has_side_effects=True),
    )(maps)
    high = pairs * HEAD
    sent = jnp.concatenate(
        [
            end_state.reshape(high, PAIR),
            jnp.pad(row_end.reshape(pairs, PAIR), ((0, 16 - pairs), (0, 0))),
        ],
        axis=0,
    )
    everyone = lax.all_gather(sent, "seq", axis=0, tiled=False)
    visible = pl.pallas_call(
        read_kernel,
        grid=(chunks,),
        in_specs=[
            pl.BlockSpec((pairs, HEAD, PAIR), lambda c: (0, 0, 0)),
            tall(),
            tall(),
            tall(),
            tall(),
            coef(),
            mats(1),
            mats(1),
        ],
        out_specs=tall(),
        out_shape=jax.ShapeDtypeStruct((tokens, width), BF16),
        scratch_shapes=[pltpu.VMEM((pairs, PAIR, PAIR), F32)],
        compiler_params=pltpu.CompilerParams(vmem_limit_bytes=48 << 20),
        cost_estimate=pl.CostEstimate(
            flops=2 * tokens * width * 1024, bytes_accessed=24 * tokens * width, transcendentals=0
        ),
    )(state_in, y, z, bonus, gating_signal, group_layernorm_coef[None], a_maps, b_maps)

    final_fold = jnp.zeros((high, PAIR), BF16)
    final_rows = jnp.zeros((1, width), BF16)
    for prompt in range(PROMPTS):
        got = lax.dynamic_index_in_dim(everyone, holders[prompt], 0, keepdims=False)
        owner = position == destination_slots[prompt]
        final_fold = jnp.where(owner, got[:high], final_fold)
        final_rows = jnp.where(owner, got[high : high + pairs].reshape(1, width), final_rows)
    final_states = final_fold.astype(F32).reshape(pairs, HEAD, 2, HEAD).transpose(0, 2, 1, 3)
    final_states = final_states.reshape(1, 2 * pairs, HEAD, HEAD)

    partial_value = jnp.dot(visible, readout_matrix, preferred_element_type=F32)
    summed = lax.psum_scatter(
        partial_value.astype(BF16), "tp", scatter_dimension=1, tiled=True
    ).astype(F32)
    mixed = (summed + layer_activation.astype(F32)).astype(BF16)
    return (mixed, final_states, final_rows)


def solution(mesh):
    return jax.shard_map(
        on_device,
        mesh=mesh,
        in_specs=(
            P("seq", "tp"),
            P("seq"),
            P(),
            P(),
            P(),
            P(),
            P(None, "tp"),
            P(None, "tp"),
            P(None, "tp"),
            P("tp", None),
            P(),
            P(None, "tp"),
            P("tp"),
            P(),
            P(None, "tp"),
            P("tp"),
            P(),
            P(None, "tp"),
            P("tp"),
            P("tp"),
            P("tp"),
            P("tp"),
        ),
        out_specs=(P("seq", "tp"), P("seq", "tp", None, None), P("seq", "tp")),
        check_vma=False,
    )
```
